1024 devices in a mesh: dp: 64 (over y, z), tensor: 16 (over x, core).
Axes of the slice: x: 8, y: 8, z: 8, core: 2. Of those that a mesh axis runs over, the one named last changes fastest.
Arguments:
- momentum: bfloat16 [64, 512, 8192], P(None, 'dp', 'tensor'), may hold values from -125 to 125
- master: float32 [64, 512, 8192], P(None, 'dp', 'tensor'), may hold values from -0.06 to 0.06
- owner_order: int32 [64], replicated, may hold values from 0 to 63, each once
Outputs:
- new_master: float32 [64, 512, 8192], P(None, 'dp', 'tensor')
- owned_update: bfloat16 [64, 512, 8192], P('dp', None, 'tensor')
The draws below stay inside these ranges and needn't reach their ends.
Inputs may be any that keep to these rules, and one draw needn't show every extreme that they name: `owner_order`: each matrix appears in exactly one slot; slot j is owned by dp index j.
All inputs are finite; a program needn't handle non-finite values.
Results may differ from the reference program's by a relative error of at most 0.025.
Values may be sent and summed in bfloat16 or wider, within the bound.
No kernel may reach another device: no remote copies, remote signals or barrier semaphores. Data moves between devices by JAX's collectives and lax.ppermute only.
A program may use at most 32 MiB of HBM per device.

```python
import math
import jax
import jax.numpy as jnp
from jax import lax

D = 8192
KV_DIM = 512
ITERS = 3
MATS = 64
COLS_DEV = 512


def draw_momentum(key, part):
    subkeys = jax.random.split(jax.random.fold_in(key, 7), 3)
    full_shape = (MATS, KV_DIM, D)
    position = jnp.arange(D, dtype=jnp.float32) / D
    entries = jnp.clip(jax.random.normal(subkeys[0], full_shape, jnp.float32), -5.0, 5.0)
    row_scale = 10.0 ** jax.random.uniform(subkeys[1], (MATS, KV_DIM, 1), jnp.float32)
    column_ramp = 3.0 ** position
    column_scale = 10.0 ** jax.random.uniform(subkeys[2], (MATS, 1, D), jnp.float32) * column_ramp[None, None, :]
    return (entries * row_scale * column_scale / 20.0).astype(jnp.bfloat16)


def shard_levels(key, extent, cuts, low, high):
    factor_of, own = 1.0, jax.random.fold_in(key, 6)
    for dim, blocks in cuts:
        heights = jnp.exp(jax.random.uniform(jax.random.fold_in(own, dim), (blocks,), jnp.float32, low / len(cuts), high / len(cuts)))
        factor_of = factor_of * jnp.repeat(heights, extent[dim] // blocks).reshape([-1 if axis == dim else 1 for axis in range(len(extent))])
    return factor_of


def centred(rng, shape, scale, reach, cuts=(), kind=jnp.bfloat16):
    drawn = scale * jax.random.normal(rng, shape, jnp.float32)
    if cuts:
        drawn = drawn * shard_levels(rng, shape, cuts, -0.22, 0.18)
    return jnp.clip(drawn, -reach, reach).astype(kind)


def setup_inputs(seed: int = 0) -> dict:
    keys = jax.random.split(jax.random.key(seed), 4)
    return {
        "momentum": draw_momentum(jax.random.fold_in(keys[3], 71), 0),
        "master": centred(keys[1], (MATS, KV_DIM, D), 0.01, 0.06, ((1, 64), (2, 16)), jnp.float32),
        "owner_order": jax.random.permutation(keys[2], MATS).astype(jnp.int32),
    }


momentum_beta_unused = 0.95
learn_rate = 0.02
weight_decay = 0.1
norm_epsilon = 1e-07
quintic_first = 3.4445
quintic_second = -4.775
quintic_third = 2.0315

def block_gram(source):
    pieces = source.reshape(KV_DIM, D // COLS_DEV, COLS_DEV).astype(jnp.float32)
    partial_value = jnp.einsum('itk,jtk->tij', pieces, pieces)
    rounded = lax.optimization_barrier(partial_value.astype(jnp.bfloat16))
    return lax.optimization_barrier(jnp.sum(rounded.astype(jnp.float32), axis=0))

def orthogonalize(matrix):
    squares = jnp.sum(jnp.square(matrix.astype(jnp.float32)))
    inv_norm = 1.0 / (jnp.sqrt(squares) + norm_epsilon)
    current = (matrix.astype(jnp.float32) * inv_norm).astype(jnp.bfloat16)
    source = matrix
    combined = current.astype(jnp.float32)
    for iteration in range(ITERS):
        gram = block_gram(source)
        if iteration == 0:
            gram = gram * (inv_norm * inv_norm)
        coupling = gram.astype(jnp.bfloat16)
        first = jnp.dot(coupling, current, preferred_element_type=jnp.float32).astype(jnp.bfloat16)
        second = jnp.dot(coupling, first, preferred_element_type=jnp.float32)
        combined = quintic_first * current.astype(jnp.float32) + quintic_second * first.astype(jnp.float32) + quintic_third * second
        if iteration + 1 < ITERS:
            current = combined.astype(jnp.bfloat16)
            source = current
    scale_out = 0.2 * math.sqrt(max(KV_DIM, D))
    return (scale_out * combined).astype(jnp.bfloat16)

def reference(momentum, master, owner_order):

    def one_slot(index):
        return orthogonalize(lax.dynamic_index_in_dim(momentum, index, 0, keepdims=False))
    owned_update = lax.map(one_slot, owner_order)
    inverse = jnp.zeros((MATS,), jnp.int32).at[owner_order].set(jnp.arange(MATS, dtype=jnp.int32))
    by_matrix = jnp.take(owned_update, inverse, axis=0)
    new_master = master * (1.0 - learn_rate * weight_decay) - learn_rate * by_matrix.astype(jnp.float32)
    return (new_master, owned_update)
```

```python
import functools
import math

import jax
import jax.numpy as jnp
from jax import lax
from jax.experimental import pallas as pl
from jax.experimental.pallas import tpu as pltpu
from jax.sharding import Mesh
from jax.sharding import PartitionSpec as P

D = 8192
KV_DIM = 512
ITERS = 3

learn_rate = 0.02
weight_decay = 0.1
norm_epsilon = 1e-07
quintic_first = 3.4445
quintic_second = -4.775
quintic_third = 2.0315
scale_out = 0.2 * math.sqrt(max(KV_DIM, D))

EDGE = 128
BLOCKS = ((0, 0), (1, 1), (2, 2), (3, 3), (0, 1), (1, 2), (2, 3), (0, 3), (0, 2), (1, 3))
HALF = len(BLOCKS) // 2
HALF_ROWS = HALF * EDGE


def matmul(left, right):
    return lax.dot_general(left, right, (((1,), (0,)), ((), ())), preferred_element_type=jnp.float32)


def two_parts(value):
    high = value.astype(jnp.bfloat16)
    return high, (value - high.astype(jnp.float32)).astype(jnp.bfloat16)


def gram_kernel(core_ref, owned_ref, kept_ref, sent_ref):
    owned = owned_ref[...]
    gram = lax.dot_general(owned, owned, (((1,), (1,)), ((), ())), preferred_element_type=jnp.float32)
    gram = gram.astype(jnp.bfloat16)
    core = core_ref[0]
    for half in range(2):
        for place in range(HALF):
            row, column = BLOCKS[half * HALF + place]
            block = gram[row * EDGE : (row + 1) * EDGE, column * EDGE : (column + 1) * EDGE]
            rows = slice(place * EDGE, (place + 1) * EDGE)

            @pl.when(core == half)
            def _(block=block, rows=rows):
                kept_ref[rows, :] = block

            @pl.when(core != half)
            def _(block=block, rows=rows):
                sent_ref[rows, :] = block


def sum_kernel(parts_ref, spread_ref):
    count = parts_ref.shape[0]
    total = parts_ref[0].astype(jnp.float32)
    for part in range(1, count):
        total = total + parts_ref[part].astype(jnp.float32)
    total = total.astype(jnp.bfloat16)
    for part in range(count):
        spread_ref[part] = total


def update_kernel(core_ref, mine_ref, other_ref, owned_ref, update_ref, gram_ref, wide_ref):
    core = core_ref[0]
    for half in range(2):
        for place in range(HALF):
            row, column = BLOCKS[half * HALF + place]
            rows = slice(place * EDGE, (place + 1) * EDGE)
            mine, other = mine_ref[rows, :].astype(jnp.float32), other_ref[rows, :].astype(jnp.float32)
            block = jnp.where(core == half, mine, other)
            down, across = pl.ds(row * EDGE, EDGE), pl.ds(column * EDGE, EDGE)
            wide_ref[down, across] = block
            if row != column:
                wide_ref[across, down] = block.T
    gram = wide_ref[...]
    gram_ref[...] = gram.astype(jnp.bfloat16)
    edge = gram.shape[0]
    diagonal = lax.broadcasted_iota(jnp.int32, (edge, edge), 0) == lax.broadcasted_iota(jnp.int32, (edge, edge), 1)
    squares = jnp.sum(jnp.where(diagonal, gram, 0.0), axis=0, keepdims=True)
    squares = jnp.sum(squares, axis=1, keepdims=True)
    inv_norm = 1.0 / (jnp.sqrt(squares) + norm_epsilon)
    inv_square = inv_norm * inv_norm

    exact = gram_ref[...]
    coupling = gram * inv_square
    square = matmul(exact, exact) * (inv_square * inv_square)
    step = quintic_second * coupling + quintic_third * square
    owned = owned_ref[...]
    current = owned.astype(jnp.float32) * inv_norm
    high, low = two_parts(step)
    current = quintic_first * current + (matmul(high, owned) + matmul(low, owned)) * inv_norm
    product = (matmul(high, exact) + matmul(low, exact)) * inv_square
    for iteration in range(1, ITERS):
        product_high, product_low = two_parts(product)
        coupling = (
            quintic_first * quintic_first * coupling
            + 2.0 * quintic_first * product
            + matmul(high, product_high)
            + matmul(high, product_low)
            + matmul(low, product_high)
        )
        coupling_high, coupling_low = two_parts(coupling)
        square = (
            matmul(coupling_high, coupling_high)
            + matmul(coupling_high, coupling_low)
            + matmul(coupling_low, coupling_high)
        )
        step = quintic_second * coupling + quintic_third * square
        high, low = two_parts(step)
        if iteration + 1 < ITERS:
            product = (
                matmul(high, coupling_high) + matmul(high, coupling_low) + matmul(low, coupling_high)
            )
        rounded = current.astype(jnp.bfloat16)
        current = quintic_first * current + matmul(high, rounded) + matmul(low, rounded)
    update_ref[...] = (scale_out * current).astype(jnp.bfloat16)


def limit(mib):
    return pltpu.CompilerParams(vmem_limit_bytes=mib * 1024 * 1024)


def vmem():
    return pl.BlockSpec(memory_space=pltpu.VMEM)


def smem():
    return pl.BlockSpec(memory_space=pltpu.SMEM)


def shards(chips, momentum, master, owner_order):
    matrices, rows, columns = momentum.shape
    slots = matrices
    core = lax.axis_index("core").astype(jnp.int32).reshape(1)
    swap = ((0, 1), (1, 0))
    slotted = jnp.take(momentum, owner_order, axis=0, mode="clip")
    owned = lax.all_to_all(slotted, "dp", split_axis=0, concat_axis=0, tiled=True)
    owned = owned.reshape(slots * rows, columns)
    packed = jax.ShapeDtypeStruct((HALF_ROWS, EDGE), jnp.bfloat16)
    kept, sent = pl.pallas_call(
        gram_kernel,
        out_shape=(packed, packed),
        in_specs=[smem(), vmem()],
        out_specs=(vmem(), vmem()),
        compiler_params=limit(8),
        name="gram",
    )(core, owned)
    received = lax.ppermute(sent, "core", swap)
    pair = (kept.astype(jnp.float32) + received.astype(jnp.float32)).astype(jnp.bfloat16)
    pair = pair.reshape(chips, HALF_ROWS // chips, EDGE)
    parts = lax.all_to_all(pair, "x", split_axis=0, concat_axis=0, tiled=True)
    spread = pl.pallas_call(
        sum_kernel,
        out_shape=jax.ShapeDtypeStruct(parts.shape, jnp.bfloat16),
        in_specs=[vmem()],
        out_specs=vmem(),
        compiler_params=limit(4),
        name="sum",
    )(parts)
    mine = lax.all_to_all(spread, "x", split_axis=0, concat_axis=0, tiled=True)
    mine = mine.reshape(HALF_ROWS, EDGE)
    other = lax.ppermute(mine, "core", swap)
    edge = owned.shape[0]
    owned_update = pl.pallas_call(
        update_kernel,
        out_shape=jax.ShapeDtypeStruct(owned.shape, jnp.bfloat16),
        in_specs=[smem(), vmem(), vmem(), vmem()],
        out_specs=vmem(),
        scratch_shapes=[
            pltpu.VMEM((edge, edge), jnp.bfloat16),
            pltpu.VMEM((edge, edge), jnp.float32),
        ],
        compiler_params=limit(24),
        name="update",
    )(core, mine, other, owned)
    returned = lax.all_to_all(
        owned_update.reshape(slots, rows, columns), "dp", split_axis=0, concat_axis=0, tiled=True
    )
    inverse = (
        jnp.zeros((matrices,), jnp.int32)
        .at[owner_order]
        .set(jnp.arange(matrices, dtype=jnp.int32), mode="promise_in_bounds", unique_indices=True)
    )
    by_matrix = jnp.take(returned, inverse, axis=0, mode="clip")
    new_master = master * (1.0 - learn_rate * weight_decay) - learn_rate * by_matrix.astype(
        jnp.float32
    )
    return (new_master, owned_update[None])


def solution(mesh):
    owners, columns = mesh.devices.shape
    chips = columns // 2
    split = Mesh(mesh.devices.reshape(owners, chips, 2), ("dp", "x", "core"))
    tensor = ("x", "core")
    return jax.shard_map(
        functools.partial(shards, chips),
        mesh=split,
        in_specs=(P(None, "dp", tensor), P(None, "dp", tensor), P()),
        out_specs=(P(None, "dp", tensor), P("dp", None, tensor)),
        check_vma=False,
    )
```

```python
import functools
import math

import jax
import jax.numpy as jnp
from jax import lax
from jax.experimental import pallas as pl
from jax.experimental.pallas import tpu as pltpu
from jax.sharding import Mesh
from jax.sharding import PartitionSpec as P

D = 8192
KV_DIM = 512
ITERS = 3

learn_rate = 0.02
weight_decay = 0.1
norm_epsilon = 1e-07
quintic_first = 3.4445
quintic_second = -4.775
quintic_third = 2.0315
scale_out = 0.2 * math.sqrt(max(KV_DIM, D))

EDGE = 128
BLOCKS = ((0, 0), (1, 1), (2, 2), (3, 3), (0, 1), (1, 2), (2, 3), (0, 3), (0, 2), (1, 3))
HALF = len(BLOCKS) // 2
HALF_ROWS = HALF * EDGE


def matmul(left, right):
    return lax.dot_general(left, right, (((1,), (0,)), ((), ())), preferred_element_type=jnp.float32)


def two_parts(value):
    high = value.astype(jnp.bfloat16)
    return high, (value - high.astype(jnp.float32)).astype(jnp.bfloat16)


def gram_kernel(core_ref, owned_ref, kept_ref, sent_ref):
    owned = owned_ref[...]
    gram = lax.dot_general(owned, owned, (((1,), (1,)), ((), ())), preferred_element_type=jnp.float32)
    gram = gram.astype(jnp.bfloat16)
    core = core_ref[0]
    for half in range(2):
        for place in range(HALF):
            row, column = BLOCKS[half * HALF + place]
            block = gram[row * EDGE : (row + 1) * EDGE, column * EDGE : (column + 1) * EDGE]
            rows = slice(place * EDGE, (place + 1) * EDGE)

            @pl.when(core == half)
            def _(block=block, rows=rows):
                kept_ref[rows, :] = block

            @pl.when(core != half)
            def _(block=block, rows=rows):
                sent_ref[rows, :] = block


def sum_kernel(parts_ref, spread_ref):
    count = parts_ref.shape[0]
    total = parts_ref[0].astype(jnp.float32)
    for part in range(1, count):
        total = total + parts_ref[part].astype(jnp.float32)
    total = total.astype(jnp.bfloat16)
    for part in range(count):
        spread_ref[part] = total


def matmuls(lefts, right):
    total = matmul(lefts[0], right)
    for left in lefts[1:]:
        total = total + matmul(left, right)
    return total


def symmetric_product(lefts, right):
    half = right.shape[0] // 2
    upper = matmuls([left[:half] for left in lefts], right)
    lower = matmuls([left[half:] for left in lefts], right[:, half:])
    return upper, lower


def whole(upper, lower):
    half = lower.shape[0]
    corner = upper[:, half:]
    left = jnp.concatenate([upper[:, :half], corner.T], axis=0)
    right = jnp.concatenate([corner, lower], axis=0)
    return jnp.concatenate([left, right], axis=1)


def update_kernel(core_ref, mine_ref, other_ref, owned_ref, update_ref, packed_ref, gram_ref):
    core = core_ref[0]
    packed_ref[pl.ds(pl.multiple_of(core * HALF_ROWS, HALF_ROWS), HALF_ROWS), :] = mine_ref[...]
    packed_ref[pl.ds(pl.multiple_of((1 - core) * HALF_ROWS, HALF_ROWS), HALF_ROWS), :] = other_ref[...]
    squares = jnp.zeros((EDGE, EDGE), jnp.float32)
    diagonal = lax.broadcasted_iota(jnp.int32, (EDGE, EDGE), 0) == lax.broadcasted_iota(jnp.int32, (EDGE, EDGE), 1)
    for place, (row, column) in enumerate(BLOCKS):
        block = packed_ref[place * EDGE : (place + 1) * EDGE, :]
        down, across = pl.ds(row * EDGE, EDGE), pl.ds(column * EDGE, EDGE)
        gram_ref[down, across] = block
        if row != column:
            gram_ref[across, down] = block.T
        else:
            squares = squares + jnp.where(diagonal, block.astype(jnp.float32), 0.0)
    squares = jnp.sum(jnp.sum(squares, axis=0, keepdims=True), axis=1, keepdims=True)
    inv_norm = 1.0 / (jnp.sqrt(squares) + norm_epsilon)
    inv_square = inv_norm * inv_norm

    gram = gram_ref[...]
    half = gram.shape[0] // 2
    coupling = (gram[:half].astype(jnp.float32) * inv_square, gram[half:, half:].astype(jnp.float32) * inv_square)
    square = symmetric_product([gram], gram)
    third = quintic_third * (inv_square * inv_square)
    step = [quintic_second * c + third * s for c, s in zip(coupling, square)]
    step = two_parts(whole(*step))
    owned = owned_ref[...]
    product = [p * inv_square for p in symmetric_product(step, gram)]
    current = quintic_first * inv_norm * owned.astype(jnp.float32) + matmuls(step, owned) * inv_norm
    for iteration in range(1, ITERS):
        high, low = two_parts(whole(*product))
        coupling = [
            quintic_first * quintic_first * c + 2.0 * quintic_first * p + (d + e)
            for c, p, d, e in zip(
                coupling, product, symmetric_product(step, high), symmetric_product(step[:1], low)
            )
        ]
        rounded = whole(*coupling).astype(jnp.bfloat16)
        square = symmetric_product([rounded], rounded)
        step = [quintic_second * c + quintic_third * s for c, s in zip(coupling, square)]
        step = two_parts(whole(*step))
        if iteration + 1 < ITERS:
            product = symmetric_product(step, rounded)
        current = quintic_first * current + matmuls(step, current.astype(jnp.bfloat16))
    update_ref[...] = (scale_out * current).astype(jnp.bfloat16)


def gather_kernel(order_ref, source_ref, slots_ref):
    def body(slot, carry):
        slots_ref[slot] = source_ref[order_ref[slot]]
        return carry

    lax.fori_loop(0, slots_ref.shape[0], body, 0, unroll=8)


def master_kernel(order_ref, returned_ref, master_ref, out_ref, ready_ref, sem):
    def body(slot, carry):
        matrix = order_ref[slot]
        ready_ref[matrix] = master_ref[matrix] * (1.0 - learn_rate * weight_decay) - learn_rate * returned_ref[
            slot
        ].astype(jnp.float32)
        pltpu.make_async_copy(ready_ref.at[matrix], out_ref.at[matrix], sem).start()
        return carry

    lax.fori_loop(0, returned_ref.shape[0], body, 0, unroll=4)
    pltpu.make_async_copy(ready_ref, out_ref, sem).wait()


def limit(mib):
    return pltpu.CompilerParams(vmem_limit_bytes=mib * 1024 * 1024)


def vmem():
    return pl.BlockSpec(memory_space=pltpu.VMEM)


def smem():
    return pl.BlockSpec(memory_space=pltpu.SMEM)


def shards(chips, momentum, master, owner_order):
    matrices, rows, columns = momentum.shape
    slots = matrices
    core = lax.axis_index("core").astype(jnp.int32).reshape(1)
    swap = ((0, 1), (1, 0))
    slotted = pl.pallas_call(
        gather_kernel,
        out_shape=jax.ShapeDtypeStruct(momentum.shape, momentum.dtype),
        in_specs=[smem(), vmem()],
        out_specs=vmem(),
        compiler_params=limit(4),
        name="gather",
    )(owner_order, momentum)
    owned = lax.all_to_all(slotted, "dp", split_axis=0, concat_axis=0, tiled=True)
    owned = owned.reshape(slots * rows, columns)
    packed = jax.ShapeDtypeStruct((HALF_ROWS, EDGE), jnp.bfloat16)
    kept, sent = pl.pallas_call(
        gram_kernel,
        out_shape=(packed, packed),
        in_specs=[smem(), vmem()],
        out_specs=(vmem(), vmem()),
        compiler_params=limit(8),
        name="gram",
    )(core, owned)
    received = lax.ppermute(sent, "core", swap)
    pair = (kept.astype(jnp.float32) + received.astype(jnp.float32)).astype(jnp.bfloat16)
    pair = pair.reshape(chips, HALF_ROWS // chips, EDGE)
    parts = lax.all_to_all(pair, "x", split_axis=0, concat_axis=0, tiled=True)
    spread = pl.pallas_call(
        sum_kernel,
        out_shape=jax.ShapeDtypeStruct(parts.shape, jnp.bfloat16),
        in_specs=[vmem()],
        out_specs=vmem(),
        compiler_params=limit(4),
        name="sum",
    )(parts)
    mine = lax.all_to_all(spread, "x", split_axis=0, concat_axis=0, tiled=True)
    mine = mine.reshape(HALF_ROWS, EDGE)
    other = lax.ppermute(mine, "core", swap)
    edge = owned.shape[0]
    owned_update = pl.pallas_call(
        update_kernel,
        out_shape=jax.ShapeDtypeStruct(owned.shape, jnp.bfloat16),
        in_specs=[smem(), vmem(), vmem(), vmem()],
        out_specs=vmem(),
        scratch_shapes=[
            pltpu.VMEM((2 * HALF_ROWS, EDGE), jnp.bfloat16),
            pltpu.VMEM((edge, edge), jnp.bfloat16),
        ],
        compiler_params=limit(24),
        name="update",
    )(core, mine, other, owned)
    returned = lax.all_to_all(
        owned_update.reshape(slots, rows, columns), "dp", split_axis=0, concat_axis=0, tiled=True
    )
    new_master = pl.pallas_call(
        master_kernel,
        out_shape=jax.ShapeDtypeStruct(master.shape, jnp.float32),
        in_specs=[smem(), vmem(), vmem()],
        out_specs=pl.BlockSpec(memory_space=pl.ANY),
        scratch_shapes=[pltpu.VMEM(master.shape, jnp.float32), pltpu.SemaphoreType.DMA],
        compiler_params=limit(8),
        name="master",
    )(owner_order, returned, master)
    return (new_master, owned_update[None])


def solution(mesh):
    owners, columns = mesh.devices.shape
    chips = columns // 2
    split = Mesh(mesh.devices.reshape(owners, chips, 2), ("dp", "x", "core"))
    tensor = ("x", "core")
    return jax.shard_map(
        functools.partial(shards, chips),
        mesh=split,
        in_specs=(P(None, "dp", tensor), P(None, "dp", tensor), P()),
        out_specs=(P(None, "dp", tensor), P("dp", None, tensor)),
        check_vma=False,
    )
```

```python
import functools
import math

import jax
import jax.numpy as jnp
from jax import lax
from jax.experimental import pallas as pl
from jax.experimental.pallas import tpu as pltpu
from jax.sharding import Mesh
from jax.sharding import PartitionSpec as P

D = 8192
KV_DIM = 512
ITERS = 3

learn_rate = 0.02
weight_decay = 0.1
norm_epsilon = 1e-07
quintic_first = 3.4445
quintic_second = -4.775
quintic_third = 2.0315
scale_out = 0.2 * math.sqrt(max(KV_DIM, D))

EDGE = 128
MID = EDGE // 2
PAIRS = ((0, 1), (1, 2), (2, 3), (0, 3), (0, 2), (1, 3))
HALF_ROWS = (3 + len(PAIRS)) * EDGE // 2


def matmul(left, right):
    return lax.dot_general(left, right, (((1,), (0,)), ((), ())), preferred_element_type=jnp.float32)


def two_parts(value):
    high = value.astype(jnp.bfloat16)
    return jnp.concatenate([high, (value - high.astype(jnp.float32)).astype(jnp.bfloat16)], axis=0)


def both(parts, right):
    rows = right.shape[0]
    product = matmul(parts, right)
    return product[:rows] + product[rows:]


def halves(core):
    return [pl.ds(pl.multiple_of(place * HALF_ROWS, HALF_ROWS), HALF_ROWS) for place in (core, 1 - core)]


def tile_masks():
    row = lax.broadcasted_iota(jnp.int32, (EDGE, EDGE), 0)
    column = lax.broadcasted_iota(jnp.int32, (EDGE, EDGE), 1)
    return row == column, (row >= MID) & (column < MID)


def gram_kernel(core_ref, owned_ref, kept_ref, sent_ref, packed_ref):
    owned = owned_ref[...]
    gram = lax.dot_general(owned, owned, (((1,), (1,)), ((), ())), preferred_element_type=jnp.float32)

    def block(row, column):
        return gram[row * EDGE : (row + 1) * EDGE, column * EDGE : (column + 1) * EDGE]

    _, lower_left = tile_masks()
    fourth = block(3, 3)
    shifted = pltpu.roll(fourth, MID, axis=1)
    quarters = (
        jnp.concatenate([fourth[MID:], fourth[:MID]], axis=0),
        jnp.concatenate([shifted[MID:], shifted[:MID]], axis=0),
        shifted,
    )
    tiles = [jnp.where(lower_left, quarter, block(place, place)) for place, quarter in enumerate(quarters)]
    tiles += [block(row, column) for row, column in PAIRS]
    for place, tile in enumerate(tiles):
        packed_ref[place * EDGE : (place + 1) * EDGE, :] = tile.astype(jnp.bfloat16)
    kept, sent = halves(core_ref[0])
    kept_ref[...] = packed_ref[kept, :]
    sent_ref[...] = packed_ref[sent, :]


def sum_kernel(parts_ref, spread_ref):
    count = parts_ref.shape[0]
    total = parts_ref[0].astype(jnp.float32)
    for part in range(1, count):
        total = total + parts_ref[part].astype(jnp.float32)
    total = total.astype(jnp.bfloat16)
    for part in range(count):
        spread_ref[part] = total


def update_kernel(core_ref, mine_ref, other_ref, owned_ref, update_ref, packed_ref, gram_ref):
    mine, other = halves(core_ref[0])
    packed_ref[mine, :] = mine_ref[...]
    packed_ref[other, :] = other_ref[...]

    def tile(place):
        return packed_ref[place * EDGE : (place + 1) * EDGE, :]

    diagonal, lower_left = tile_masks()
    blocks = [tile(place).astype(jnp.float32) for place in range(3)]
    left = lax.broadcasted_iota(jnp.int32, (MID, EDGE), 1) < MID
    first, second, third = (block[MID:] for block in blocks)
    upper = jnp.where(left, first, pltpu.roll(second, MID, axis=1))
    blocks.append(jnp.concatenate([upper, pltpu.roll(third, MID, axis=1)], axis=0))
    squares = jnp.where(diagonal, blocks[0] + blocks[1] + blocks[2] + blocks[3], 0.0)
    for place, block in enumerate(blocks):
        at = pl.ds(place * EDGE, EDGE)
        gram_ref[at, at] = jnp.where(lower_left, block.T, block).astype(jnp.bfloat16)
    for place, (row, column) in enumerate(PAIRS):
        block = tile(3 + place)
        down, across = pl.ds(row * EDGE, EDGE), pl.ds(column * EDGE, EDGE)
        gram_ref[down, across] = block
        gram_ref[across, down] = block.T
    squares = jnp.sum(jnp.sum(squares, axis=0, keepdims=True), axis=1, keepdims=True)
    inv_norm = 1.0 / (jnp.sqrt(squares) + norm_epsilon)
    inv_square = inv_norm * inv_norm

    factor = gram_ref[...]
    edge = factor.shape[0]
    coupling = factor.astype(jnp.float32) * inv_square
    square = matmul(factor, factor) * (inv_square * inv_square)
    step = two_parts(quintic_second * coupling + quintic_third * square)
    product = both(step, factor) * inv_square
    owned = owned_ref[...]
    current = (quintic_first * owned.astype(jnp.float32) + both(step, owned)) * inv_norm
    for iteration in range(1, ITERS):
        parts = two_parts(product)
        coupling = (
            quintic_first * quintic_first * coupling
            + 2.0 * quintic_first * product
            + both(step, parts[:edge])
            + matmul(step[:edge], parts[edge:])
        )
        factor = coupling.astype(jnp.bfloat16)
        square = matmul(factor, factor)
        step = two_parts(quintic_second * coupling + quintic_third * square)
        if iteration + 1 < ITERS:
            product = both(step, factor)
        current = quintic_first * current + both(step, current.astype(jnp.bfloat16))
    update_ref[...] = (scale_out * current).astype(jnp.bfloat16)


def gather_kernel(order_ref, source_ref, slots_ref):
    def body(slot, carry):
        slots_ref[slot] = source_ref[order_ref[slot]]
        return carry

    lax.fori_loop(0, slots_ref.shape[0], body, 0, unroll=8)


def master_kernel(order_ref, returned_ref, master_ref, out_ref, ready_ref, sem):
    def body(slot, carry):
        matrix = order_ref[slot]
        ready_ref[matrix] = master_ref[matrix] * (1.0 - learn_rate * weight_decay) - learn_rate * returned_ref[
            slot
        ].astype(jnp.float32)
        pltpu.make_async_copy(ready_ref.at[matrix], out_ref.at[matrix], sem).start()
        return carry

    lax.fori_loop(0, returned_ref.shape[0], body, 0, unroll=4)
    pltpu.make_async_copy(ready_ref, out_ref, sem).wait()


def limit(mib):
    return pltpu.CompilerParams(vmem_limit_bytes=mib * 1024 * 1024)


def vmem():
    return pl.BlockSpec(memory_space=pltpu.VMEM)


def smem():
    return pl.BlockSpec(memory_space=pltpu.SMEM)


def shards(chips, momentum, master, owner_order):
    matrices, rows, columns = momentum.shape
    slots = matrices
    core = lax.axis_index("core").astype(jnp.int32).reshape(1)
    swap = ((0, 1), (1, 0))
    slotted = pl.pallas_call(
        gather_kernel,
        out_shape=jax.ShapeDtypeStruct(momentum.shape, momentum.dtype),
        in_specs=[smem(), vmem()],
        out_specs=vmem(),
        name="gather",
    )(owner_order, momentum)
    owned = lax.all_to_all(slotted, "dp", split_axis=0, concat_axis=0, tiled=True)
    owned = owned.reshape(slots * rows, columns)
    packed = jax.ShapeDtypeStruct((HALF_ROWS, EDGE), jnp.bfloat16)
    kept, sent = pl.pallas_call(
        gram_kernel,
        out_shape=(packed, packed),
        in_specs=[smem(), vmem()],
        out_specs=(vmem(), vmem()),
        scratch_shapes=[pltpu.VMEM((2 * HALF_ROWS, EDGE), jnp.bfloat16)],
        compiler_params=limit(8),
        name="gram",
    )(core, owned)
    received = lax.ppermute(sent, "core", swap)
    pair = (kept.astype(jnp.float32) + received.astype(jnp.float32)).astype(jnp.bfloat16)
    pair = pair.reshape(chips, HALF_ROWS // chips, EDGE)
    parts = lax.all_to_all(pair, "x", split_axis=0, concat_axis=0, tiled=True)
    spread = pl.pallas_call(
        sum_kernel,
        out_shape=jax.ShapeDtypeStruct(parts.shape, jnp.bfloat16),
        in_specs=[vmem()],
        out_specs=vmem(),
        compiler_params=limit(4),
        name="sum",
    )(parts)
    mine = lax.all_to_all(spread, "x", split_axis=0, concat_axis=0, tiled=True)
    mine = mine.reshape(HALF_ROWS, EDGE)
    other = lax.ppermute(mine, "core", swap)
    edge = owned.shape[0]
    owned_update = pl.pallas_call(
        update_kernel,
        out_shape=jax.ShapeDtypeStruct(owned.shape, jnp.bfloat16),
        in_specs=[smem(), vmem(), vmem(), vmem()],
        out_specs=vmem(),
        scratch_shapes=[
            pltpu.VMEM((2 * HALF_ROWS, EDGE), jnp.bfloat16),
            pltpu.VMEM((edge, edge), jnp.bfloat16),
        ],
        compiler_params=limit(24),
        name="update",
    )(core, mine, other, owned)
    returned = lax.all_to_all(
        owned_update.reshape(slots, rows, columns), "dp", split_axis=0, concat_axis=0, tiled=True
    )
    new_master = pl.pallas_call(
        master_kernel,
        out_shape=jax.ShapeDtypeStruct(master.shape, jnp.float32),
        in_specs=[smem(), vmem(), vmem()],
        out_specs=pl.BlockSpec(memory_space=pl.ANY),
        scratch_shapes=[pltpu.VMEM(master.shape, jnp.float32), pltpu.SemaphoreType.DMA],
        compiler_params=limit(8),
        name="master",
    )(owner_order, returned, master)
    return (new_master, owned_update[None])


def solution(mesh):
    owners, columns = mesh.devices.shape
    chips = columns // 2
    split = Mesh(mesh.devices.reshape(owners, chips, 2), ("dp", "x", "core"))
    tensor = ("x", "core")
    return jax.shard_map(
        functools.partial(shards, chips),
        mesh=split,
        in_specs=(P(None, "dp", tensor), P(None, "dp", tensor), P()),
        out_specs=(P(None, "dp", tensor), P("dp", None, tensor)),
        check_vma=False,
    )
```

```python
import functools
import math

import jax
import jax.numpy as jnp
from jax import lax
from jax.experimental import pallas as pl
from jax.experimental.pallas import tpu as pltpu
from jax.sharding import Mesh
from jax.sharding import PartitionSpec as P

D = 8192
KV_DIM = 512
ITERS = 3

learn_rate = 0.02
weight_decay = 0.1
norm_epsilon = 1e-07
quintic_first = 3.4445
quintic_second = -4.775
quintic_third = 2.0315
scale_out = 0.2 * math.sqrt(max(KV_DIM, D))

EDGE = 128
MID = EDGE // 2
PAIRS = ((0, 1), (1, 2), (2, 3), (0, 3), (0, 2), (1, 3))
HALF_ROWS = (3 + len(PAIRS)) * EDGE // 2


def matmul(left, right):
    return lax.dot_general(left, right, (((1,), (0,)), ((), ())), preferred_element_type=jnp.float32)


def two_parts(value):
    high = value.astype(jnp.bfloat16)
    return high, (value - high.astype(jnp.float32)).astype(jnp.bfloat16)


def matmuls(lefts, right):
    total = matmul(lefts[0], right)
    for left in lefts[1:]:
        total = total + matmul(left, right)
    return total


def symmetric_product(lefts, right):
    half = right.shape[0] // 2
    upper = matmuls([left[:half] for left in lefts], right)
    lower = matmuls([left[half:] for left in lefts], right[:, half:])
    return upper, lower


def whole(upper, lower):
    half = lower.shape[0]
    corner = upper[:, half:]
    left = jnp.concatenate([upper[:, :half], corner.T], axis=0)
    right = jnp.concatenate([corner, lower], axis=0)
    return jnp.concatenate([left, right], axis=1)


def halves(core):
    return [pl.ds(pl.multiple_of(place * HALF_ROWS, HALF_ROWS), HALF_ROWS) for place in (core, 1 - core)]


def tile_masks():
    row = lax.broadcasted_iota(jnp.int32, (EDGE, EDGE), 0)
    column = lax.broadcasted_iota(jnp.int32, (EDGE, EDGE), 1)
    return row == column, (row >= MID) & (column < MID)


def gram_kernel(core_ref, owned_ref, kept_ref, sent_ref, packed_ref):
    owned = owned_ref[...]
    gram = lax.dot_general(owned, owned, (((1,), (1,)), ((), ())), preferred_element_type=jnp.float32)

    def block(row, column):
        return gram[row * EDGE : (row + 1) * EDGE, column * EDGE : (column + 1) * EDGE]

    _, lower_left = tile_masks()
    fourth = block(3, 3)
    shifted = pltpu.roll(fourth, MID, axis=1)
    quarters = (
        jnp.concatenate([fourth[MID:], fourth[:MID]], axis=0),
        jnp.concatenate([shifted[MID:], shifted[:MID]], axis=0),
        shifted,
    )
    tiles = [jnp.where(lower_left, quarter, block(place, place)) for place, quarter in enumerate(quarters)]
    tiles += [block(row, column) for row, column in PAIRS]
    for place, tile in enumerate(tiles):
        packed_ref[place * EDGE : (place + 1) * EDGE, :] = tile.astype(jnp.bfloat16)
    kept, sent = halves(core_ref[0])
    kept_ref[...] = packed_ref[kept, :]
    sent_ref[...] = packed_ref[sent, :]


def sum_kernel(parts_ref, spread_ref):
    count = parts_ref.shape[0]
    total = parts_ref[0].astype(jnp.float32)
    for part in range(1, count):
        total = total + parts_ref[part].astype(jnp.float32)
    total = total.astype(jnp.bfloat16)
    for part in range(count):
        spread_ref[part] = total


def update_kernel(core_ref, mine_ref, other_ref, owned_ref, update_ref, packed_ref, gram_ref):
    mine, other = halves(core_ref[0])
    packed_ref[mine, :] = mine_ref[...]
    packed_ref[other, :] = other_ref[...]

    def tile(place):
        return packed_ref[place * EDGE : (place + 1) * EDGE, :]

    diagonal, lower_left = tile_masks()
    blocks = [tile(place).astype(jnp.float32) for place in range(3)]
    left = lax.broadcasted_iota(jnp.int32, (MID, EDGE), 1) < MID
    first, second, third = (block[MID:] for block in blocks)
    upper = jnp.where(left, first, pltpu.roll(second, MID, axis=1))
    blocks.append(jnp.concatenate([upper, pltpu.roll(third, MID, axis=1)], axis=0))
    squares = jnp.where(diagonal, blocks[0] + blocks[1] + blocks[2] + blocks[3], 0.0)
    for place, block in enumerate(blocks):
        at = pl.ds(place * EDGE, EDGE)
        gram_ref[at, at] = jnp.where(lower_left, block.T, block).astype(jnp.bfloat16)
    for place, (row, column) in enumerate(PAIRS):
        block = tile(3 + place)
        down, across = pl.ds(row * EDGE, EDGE), pl.ds(column * EDGE, EDGE)
        gram_ref[down, across] = block
        gram_ref[across, down] = block.T
    squares = jnp.sum(jnp.sum(squares, axis=0, keepdims=True), axis=1, keepdims=True)
    inv_norm = 1.0 / (jnp.sqrt(squares) + norm_epsilon)
    inv_square = inv_norm * inv_norm

    factor = gram_ref[...]
    half = factor.shape[0] // 2
    coupling = [
        factor[:half].astype(jnp.float32) * inv_square,
        factor[half:, half:].astype(jnp.float32) * inv_square,
    ]
    square = symmetric_product([factor], factor)
    third = quintic_third * (inv_square * inv_square)
    step = [quintic_second * c + third * s for c, s in zip(coupling, square)]
    step = two_parts(whole(*step))
    operand = owned_ref[...]
    product = [p * inv_square for p in symmetric_product(step, factor)]
    current = (quintic_first * operand.astype(jnp.float32) + matmul(step[0], operand)) * inv_norm
    rest_scale = inv_norm
    for iteration in range(1, ITERS):
        high, low = two_parts(whole(*product))
        coupling = [
            quintic_first * quintic_first * c + 2.0 * quintic_first * p + (d + e)
            for c, p, d, e in zip(
                coupling, product, symmetric_product(step, high), symmetric_product(step[:1], low)
            )
        ]
        current = current + matmul(step[1], operand) * rest_scale
        operand = current.astype(jnp.bfloat16)
        factor = whole(*coupling).astype(jnp.bfloat16)
        if iteration + 1 < ITERS:
            square = symmetric_product([factor], factor)
            step = [quintic_second * c + quintic_third * s for c, s in zip(coupling, square)]
            step = two_parts(whole(*step))
            product = symmetric_product(step, factor)
            current = quintic_first * current + matmul(step[0], operand)
            rest_scale = 1.0
    first = matmul(factor, operand).astype(jnp.bfloat16)
    for rows in (slice(0, half), slice(half, 2 * half)):
        second = matmul(factor[rows], first)
        update = quintic_first * current[rows] + quintic_second * first[rows].astype(jnp.float32) + quintic_third * second
        update_ref[rows, :] = (scale_out * update).astype(jnp.bfloat16)


def gather_kernel(order_ref, source_ref, slots_ref):
    def body(slot, carry):
        slots_ref[slot] = source_ref[order_ref[slot]]
        return carry

    lax.fori_loop(0, slots_ref.shape[0], body, 0, unroll=8)


def master_kernel(order_ref, returned_ref, master_ref, out_ref, ready_ref, sem):
    def body(slot, carry):
        matrix = order_ref[slot]
        ready_ref[matrix] = master_ref[matrix] * (1.0 - learn_rate * weight_decay) - learn_rate * returned_ref[
            slot
        ].astype(jnp.float32)
        pltpu.make_async_copy(ready_ref.at[matrix], out_ref.at[matrix], sem).start()
        return carry

    lax.fori_loop(0, returned_ref.shape[0], body, 0, unroll=4)
    pltpu.make_async_copy(ready_ref, out_ref, sem).wait()


def limit(mib):
    return pltpu.CompilerParams(vmem_limit_bytes=mib * 1024 * 1024)


def vmem():
    return pl.BlockSpec(memory_space=pltpu.VMEM)


def smem():
    return pl.BlockSpec(memory_space=pltpu.SMEM)


def shards(chips, momentum, master, owner_order):
    matrices, rows, columns = momentum.shape
    slots = matrices
    core = lax.axis_index("core").astype(jnp.int32).reshape(1)
    swap = ((0, 1), (1, 0))
    slotted = pl.pallas_call(
        gather_kernel,
        out_shape=jax.ShapeDtypeStruct(momentum.shape, momentum.dtype),
        in_specs=[smem(), vmem()],
        out_specs=vmem(),
        name="gather",
    )(owner_order, momentum)
    owned = lax.all_to_all(slotted, "dp", split_axis=0, concat_axis=0, tiled=True)
    owned = owned.reshape(slots * rows, columns)
    packed = jax.ShapeDtypeStruct((HALF_ROWS, EDGE), jnp.bfloat16)
    kept, sent = pl.pallas_call(
        gram_kernel,
        out_shape=(packed, packed),
        in_specs=[smem(), vmem()],
        out_specs=(vmem(), vmem()),
        scratch_shapes=[pltpu.VMEM((2 * HALF_ROWS, EDGE), jnp.bfloat16)],
        compiler_params=limit(8),
        name="gram",
    )(core, owned)
    received = lax.ppermute(sent, "core", swap)
    pair = (kept.astype(jnp.float32) + received.astype(jnp.float32)).astype(jnp.bfloat16)
    pair = pair.reshape(chips, HALF_ROWS // chips, EDGE)
    parts = lax.all_to_all(pair, "x", split_axis=0, concat_axis=0, tiled=True)
    spread = pl.pallas_call(
        sum_kernel,
        out_shape=jax.ShapeDtypeStruct(parts.shape, jnp.bfloat16),
        in_specs=[vmem()],
        out_specs=vmem(),
        compiler_params=limit(4),
        name="sum",
    )(parts)
    mine = lax.all_to_all(spread, "x", split_axis=0, concat_axis=0, tiled=True)
    mine = mine.reshape(HALF_ROWS, EDGE)
    other = lax.ppermute(mine, "core", swap)
    edge = owned.shape[0]
    owned_update = pl.pallas_call(
        update_kernel,
        out_shape=jax.ShapeDtypeStruct(owned.shape, jnp.bfloat16),
        in_specs=[smem(), vmem(), vmem(), vmem()],
        out_specs=vmem(),
        scratch_shapes=[
            pltpu.VMEM((2 * HALF_ROWS, EDGE), jnp.bfloat16),
            pltpu.VMEM((edge, edge), jnp.bfloat16),
        ],
        compiler_params=limit(24),
        name="update",
    )(core, mine, other, owned)
    returned = lax.all_to_all(
        owned_update.reshape(slots, rows, columns), "dp", split_axis=0, concat_axis=0, tiled=True
    )
    new_master = pl.pallas_call(
        master_kernel,
        out_shape=jax.ShapeDtypeStruct(master.shape, jnp.float32),
        in_specs=[smem(), vmem(), vmem()],
        out_specs=pl.BlockSpec(memory_space=pl.ANY),
        scratch_shapes=[pltpu.VMEM(master.shape, jnp.float32), pltpu.SemaphoreType.DMA],
        compiler_params=limit(8),
        name="master",
    )(owner_order, returned, master)
    return (new_master, owned_update[None])


def solution(mesh):
    owners, columns = mesh.devices.shape
    chips = columns // 2
    split = Mesh(mesh.devices.reshape(owners, chips, 2), ("dp", "x", "core"))
    tensor = ("x", "core")
    return jax.shard_map(
        functools.partial(shards, chips),
        mesh=split,
        in_specs=(P(None, "dp", tensor), P(None, "dp", tensor), P()),
        out_specs=(P(None, "dp", tensor), P("dp", None, tensor)),
        check_vma=False,
    )
```

```python
import functools
import math

import jax
import jax.numpy as jnp
from jax import lax
from jax.experimental import pallas as pl
from jax.experimental.pallas import tpu as pltpu
from jax.sharding import Mesh
from jax.sharding import PartitionSpec as P

D = 8192
KV_DIM = 512
ITERS = 3

learn_rate = 0.02
weight_decay = 0.1
norm_epsilon = 1e-07
quintic_first = 3.4445
quintic_second = -4.775
quintic_third = 2.0315
scale_out = 0.2 * math.sqrt(max(KV_DIM, D))

EDGE = 128
MID = EDGE // 2
PAIRS = ((0, 1), (1, 2), (2, 3), (0, 3), (0, 2), (1, 3))
HALF_ROWS = (3 + len(PAIRS)) * EDGE // 2


def matmul(left, right):
    return lax.dot_general(left, right, (((1,), (0,)), ((), ())), preferred_element_type=jnp.float32)


def two_parts(value):
    high = value.astype(jnp.bfloat16)
    return high, (value - high.astype(jnp.float32)).astype(jnp.bfloat16)


def matmuls(lefts, right):
    total = matmul(lefts[0], right)
    for left in lefts[1:]:
        total = total + matmul(left, right)
    return total


def symmetric_product(lefts, right):
    half = right.shape[0] // 2
    upper = matmuls([left[:half] for left in lefts], right)
    lower = matmuls([left[half:] for left in lefts], right[:, half:])
    return upper, lower


def whole(upper, lower):
    half = lower.shape[0]
    corner = upper[:, half:]
    left = jnp.concatenate([upper[:, :half], corner.T], axis=0)
    right = jnp.concatenate([corner, lower], axis=0)
    return jnp.concatenate([left, right], axis=1)


def halves(core):
    return [pl.ds(pl.multiple_of(place * HALF_ROWS, HALF_ROWS), HALF_ROWS) for place in (core, 1 - core)]


def tile_masks():
    row = lax.broadcasted_iota(jnp.int32, (EDGE, EDGE), 0)
    column = lax.broadcasted_iota(jnp.int32, (EDGE, EDGE), 1)
    return row == column, (row >= MID) & (column < MID)


def gram_kernel(core_ref, owned_ref, kept_ref, sent_ref, packed_ref):
    owned = owned_ref[...]
    gram = lax.dot_general(owned, owned, (((1,), (1,)), ((), ())), preferred_element_type=jnp.float32)

    def block(row, column):
        return gram[row * EDGE : (row + 1) * EDGE, column * EDGE : (column + 1) * EDGE]

    _, lower_left = tile_masks()
    fourth = block(3, 3)
    shifted = pltpu.roll(fourth, MID, axis=1)
    quarters = (
        jnp.concatenate([fourth[MID:], fourth[:MID]], axis=0),
        jnp.concatenate([shifted[MID:], shifted[:MID]], axis=0),
        shifted,
    )
    tiles = [jnp.where(lower_left, quarter, block(place, place)) for place, quarter in enumerate(quarters)]
    tiles += [block(row, column) for row, column in PAIRS]
    for place, tile in enumerate(tiles):
        packed_ref[place * EDGE : (place + 1) * EDGE, :] = tile.astype(jnp.bfloat16)
    kept, sent = halves(core_ref[0])
    kept_ref[...] = packed_ref[kept, :]
    sent_ref[...] = packed_ref[sent, :]


def sum_kernel(parts_ref, spread_ref):
    count = parts_ref.shape[0]
    total = parts_ref[0].astype(jnp.float32)
    for part in range(1, count):
        total = total + parts_ref[part].astype(jnp.float32)
    total = total.astype(jnp.bfloat16)
    for part in range(count):
        spread_ref[part] = total


def update_kernel(core_ref, mine_ref, other_ref, owned_ref, update_ref, packed_ref, gram_ref):
    mine, other = halves(core_ref[0])
    packed_ref[mine, :] = mine_ref[...]
    packed_ref[other, :] = other_ref[...]

    def tile(place):
        return packed_ref[place * EDGE : (place + 1) * EDGE, :]

    diagonal, lower_left = tile_masks()
    blocks = [tile(place).astype(jnp.float32) for place in range(3)]
    left = lax.broadcasted_iota(jnp.int32, (MID, EDGE), 1) < MID
    first, second, third = (block[MID:] for block in blocks)
    upper = jnp.where(left, first, pltpu.roll(second, MID, axis=1))
    blocks.append(jnp.concatenate([upper, pltpu.roll(third, MID, axis=1)], axis=0))
    squares = jnp.where(diagonal, blocks[0] + blocks[1] + blocks[2] + blocks[3], 0.0)
    for place, block in enumerate(blocks):
        at = pl.ds(place * EDGE, EDGE)
        gram_ref[at, at] = jnp.where(lower_left, block.T, block).astype(jnp.bfloat16)
    for place, (row, column) in enumerate(PAIRS):
        block = tile(3 + place)
        down, across = pl.ds(row * EDGE, EDGE), pl.ds(column * EDGE, EDGE)
        gram_ref[down, across] = block
        gram_ref[across, down] = block.T
    squares = jnp.sum(jnp.sum(squares, axis=0, keepdims=True), axis=1, keepdims=True)
    inv_norm = 1.0 / (jnp.sqrt(squares) + norm_epsilon)
    inv_square = inv_norm * inv_norm

    factor = gram_ref[...]
    half = factor.shape[0] // 2
    coupling = [
        factor[:half].astype(jnp.float32) * inv_square,
        factor[half:, half:].astype(jnp.float32) * inv_square,
    ]
    square = symmetric_product([factor], factor)
    third = quintic_third * (inv_square * inv_square)
    step = [quintic_second * c + third * s for c, s in zip(coupling, square)]
    step = two_parts(whole(*step))
    operand = owned_ref[...]
    product = [p * inv_square for p in symmetric_product(step, factor)]
    current = (quintic_first * operand.astype(jnp.float32) + matmul(step[0], operand)) * inv_norm
    rest_scale = inv_norm
    for iteration in range(1, ITERS):
        high, low = two_parts(whole(*product))
        coupling = [
            quintic_first * quintic_first * c + 2.0 * quintic_first * p + (d + e)
            for c, p, d, e in zip(
                coupling, product, symmetric_product(step, high), symmetric_product(step[:1], low)
            )
        ]
        current = current + matmul(step[1], operand) * rest_scale
        operand = current.astype(jnp.bfloat16)
        factor = whole(*coupling).astype(jnp.bfloat16)
        if iteration + 1 < ITERS:
            square = symmetric_product([factor], factor)
            step = [quintic_second * c + quintic_third * s for c, s in zip(coupling, square)]
            step = two_parts(whole(*step))
            product = symmetric_product(step, factor)
            current = quintic_first * current + matmul(step[0], operand)
            rest_scale = 1.0
    first = matmul(factor, operand).astype(jnp.bfloat16)
    for rows in (slice(0, half), slice(half, 2 * half)):
        second = matmul(factor[rows], first)
        update = quintic_first * current[rows] + quintic_second * first[rows].astype(jnp.float32) + quintic_third * second
        update_ref[rows, :] = (scale_out * update).astype(jnp.bfloat16)


def gather_kernel(order_ref, source_ref, slots_ref):
    def body(slot, carry):
        slots_ref[slot] = source_ref[order_ref[slot]]
        return carry

    lax.fori_loop(0, slots_ref.shape[0], body, 0, unroll=8)


def master_kernel(order_ref, returned_ref, master_ref, update_ref, out_ref, owned_ref, ready_ref, sem, owned_sem):
    owned = pltpu.make_async_copy(update_ref, owned_ref, owned_sem)
    owned.start()

    def body(slot, carry):
        matrix = order_ref[slot]
        ready_ref[matrix] = master_ref[matrix] * (1.0 - learn_rate * weight_decay) - learn_rate * returned_ref[
            slot
        ].astype(jnp.float32)
        pltpu.make_async_copy(ready_ref.at[matrix], out_ref.at[matrix], sem).start()
        return carry

    lax.fori_loop(0, returned_ref.shape[0], body, 0, unroll=4)
    pltpu.make_async_copy(ready_ref, out_ref, sem).wait()
    owned.wait()


def limit(mib):
    return pltpu.CompilerParams(vmem_limit_bytes=mib * 1024 * 1024)


def vmem():
    return pl.BlockSpec(memory_space=pltpu.VMEM)


def smem():
    return pl.BlockSpec(memory_space=pltpu.SMEM)


def shards(chips, momentum, master, owner_order):
    matrices, rows, columns = momentum.shape
    slots = matrices
    core = lax.axis_index("core").astype(jnp.int32).reshape(1)
    swap = ((0, 1), (1, 0))
    slotted = pl.pallas_call(
        gather_kernel,
        out_shape=jax.ShapeDtypeStruct(momentum.shape, momentum.dtype),
        in_specs=[smem(), vmem()],
        out_specs=vmem(),
        compiler_params=limit(53),
        name="gather",
    )(owner_order, momentum)
    core, slotted = lax.optimization_barrier((core, slotted))
    owned = lax.all_to_all(slotted, "dp", split_axis=0, concat_axis=0, tiled=True)
    owned = owned.reshape(slots * rows, columns)
    packed = jax.ShapeDtypeStruct((HALF_ROWS, EDGE), jnp.bfloat16)
    kept, sent = pl.pallas_call(
        gram_kernel,
        out_shape=(packed, packed),
        in_specs=[smem(), vmem()],
        out_specs=(vmem(), vmem()),
        scratch_shapes=[pltpu.VMEM((2 * HALF_ROWS, EDGE), jnp.bfloat16)],
        compiler_params=limit(8),
        name="gram",
    )(core, owned)
    received = lax.ppermute(sent, "core", swap)
    pair = (kept.astype(jnp.float32) + received.astype(jnp.float32)).astype(jnp.bfloat16)
    pair = pair.reshape(chips, HALF_ROWS // chips, EDGE)
    parts = lax.all_to_all(pair, "x", split_axis=0, concat_axis=0, tiled=True)
    spread = pl.pallas_call(
        sum_kernel,
        out_shape=jax.ShapeDtypeStruct(parts.shape, jnp.bfloat16),
        in_specs=[vmem()],
        out_specs=vmem(),
        compiler_params=limit(4),
        name="sum",
    )(parts)
    mine = lax.all_to_all(spread, "x", split_axis=0, concat_axis=0, tiled=True)
    mine = mine.reshape(HALF_ROWS, EDGE)
    other = lax.ppermute(mine, "core", swap)
    edge = owned.shape[0]
    update = pl.pallas_call(
        update_kernel,
        out_shape=jax.ShapeDtypeStruct(owned.shape, jnp.bfloat16),
        in_specs=[smem(), vmem(), vmem(), vmem()],
        out_specs=vmem(),
        scratch_shapes=[
            pltpu.VMEM((2 * HALF_ROWS, EDGE), jnp.bfloat16),
            pltpu.VMEM((edge, edge), jnp.bfloat16),
        ],
        compiler_params=limit(24),
        name="update",
    )(core, mine, other, owned)
    returned = lax.all_to_all(
        update.reshape(slots, rows, columns), "dp", split_axis=0, concat_axis=0, tiled=True
    )
    new_master, owned_update = pl.pallas_call(
        master_kernel,
        out_shape=(
            jax.ShapeDtypeStruct(master.shape, jnp.float32),
            jax.ShapeDtypeStruct(update.shape, update.dtype),
        ),
        in_specs=[smem(), vmem(), vmem(), vmem()],
        out_specs=(pl.BlockSpec(memory_space=pl.ANY),) * 2,
        scratch_shapes=[
            pltpu.VMEM(master.shape, jnp.float32),
            pltpu.SemaphoreType.DMA,
            pltpu.SemaphoreType.DMA,
        ],
        compiler_params=limit(8),
        name="master",
    )(owner_order, returned, master, update)
    return (new_master, owned_update[None])


def solution(mesh):
    owners, columns = mesh.devices.shape
    chips = columns // 2
    split = Mesh(mesh.devices.reshape(owners, chips, 2), ("dp", "x", "core"))
    tensor = ("x", "core")
    return jax.shard_map(
        functools.partial(shards, chips),
        mesh=split,
        in_specs=(P(None, "dp", tensor), P(None, "dp", tensor), P()),
        out_specs=(P(None, "dp", tensor), P("dp", None, tensor)),
        check_vma=False,
    )
```

```python
import functools
import math

import jax
import jax.numpy as jnp
from jax import lax
from jax.experimental import pallas as pl
from jax.experimental.pallas import tpu as pltpu
from jax.sharding import Mesh
from jax.sharding import PartitionSpec as P

D = 8192
KV_DIM = 512
ITERS = 3

learn_rate = 0.02
weight_decay = 0.1
norm_epsilon = 1e-07
quintic_first = 3.4445
quintic_second = -4.775
quintic_third = 2.0315
scale_out = 0.2 * math.sqrt(max(KV_DIM, D))

EDGE = 128
MID = EDGE // 2
PAIRS = ((0, 1), (1, 2), (2, 3), (0, 3), (0, 2), (1, 3))
HALF_ROWS = (3 + len(PAIRS)) * EDGE // 2


def matmul(left, right):
    return lax.dot_general(left, right, (((1,), (0,)), ((), ())), preferred_element_type=jnp.float32)


def two_parts(value):
    high = value.astype(jnp.bfloat16)
    return high, (value - high.astype(jnp.float32)).astype(jnp.bfloat16)


def matmuls(lefts, right):
    total = matmul(lefts[0], right)
    for left in lefts[1:]:
        total = total + matmul(left, right)
    return total


def symmetric_product(lefts, right):
    half = right.shape[0] // 2
    upper = matmuls([left[:half] for left in lefts], right)
    lower = matmuls([left[half:] for left in lefts], right[:, half:])
    return upper, lower


def whole(upper, lower):
    half = lower.shape[0]
    corner = upper[:, half:]
    left = jnp.concatenate([upper[:, :half], corner.T], axis=0)
    right = jnp.concatenate([corner, lower], axis=0)
    return jnp.concatenate([left, right], axis=1)


def halves(core):
    return [pl.ds(pl.multiple_of(place * HALF_ROWS, HALF_ROWS), HALF_ROWS) for place in (core, 1 - core)]


def tile_masks():
    row = lax.broadcasted_iota(jnp.int32, (EDGE, EDGE), 0)
    column = lax.broadcasted_iota(jnp.int32, (EDGE, EDGE), 1)
    return row == column, (row >= MID) & (column < MID)


def gram_kernel(core_ref, owned_ref, kept_ref, sent_ref, packed_ref):
    owned = owned_ref[...]
    gram = lax.dot_general(owned, owned, (((1,), (1,)), ((), ())), preferred_element_type=jnp.float32)

    def block(row, column):
        return gram[row * EDGE : (row + 1) * EDGE, column * EDGE : (column + 1) * EDGE]

    _, lower_left = tile_masks()
    fourth = block(3, 3)
    shifted = pltpu.roll(fourth, MID, axis=1)
    quarters = (
        jnp.concatenate([fourth[MID:], fourth[:MID]], axis=0),
        jnp.concatenate([shifted[MID:], shifted[:MID]], axis=0),
        shifted,
    )
    tiles = [jnp.where(lower_left, quarter, block(place, place)) for place, quarter in enumerate(quarters)]
    tiles += [block(row, column) for row, column in PAIRS]
    for place, tile in enumerate(tiles):
        packed_ref[place * EDGE : (place + 1) * EDGE, :] = tile.astype(jnp.bfloat16)
    kept, sent = halves(core_ref[0])
    kept_ref[...] = packed_ref[kept, :]
    sent_ref[...] = packed_ref[sent, :]


def sum_kernel(parts_ref, spread_ref):
    count = parts_ref.shape[0]
    total = parts_ref[0].astype(jnp.float32)
    for part in range(1, count):
        total = total + parts_ref[part].astype(jnp.float32)
    total = total.astype(jnp.bfloat16)
    for part in range(count):
        spread_ref[part] = total


def update_kernel(core_ref, mine_ref, other_ref, owned_ref, update_ref, packed_ref, gram_ref):
    mine, other = halves(core_ref[0])
    packed_ref[mine, :] = mine_ref[...]
    packed_ref[other, :] = other_ref[...]

    def tile(place):
        return packed_ref[place * EDGE : (place + 1) * EDGE, :]

    diagonal, lower_left = tile_masks()
    blocks = [tile(place).astype(jnp.float32) for place in range(3)]
    left = lax.broadcasted_iota(jnp.int32, (MID, EDGE), 1) < MID
    first, second, third = (block[MID:] for block in blocks)
    upper = jnp.where(left, first, pltpu.roll(second, MID, axis=1))
    blocks.append(jnp.concatenate([upper, pltpu.roll(third, MID, axis=1)], axis=0))
    squares = jnp.where(diagonal, blocks[0] + blocks[1] + blocks[2] + blocks[3], 0.0)
    for place, block in enumerate(blocks):
        at = pl.ds(place * EDGE, EDGE)
        gram_ref[at, at] = jnp.where(lower_left, block.T, block).astype(jnp.bfloat16)
    for place, (row, column) in enumerate(PAIRS):
        block = tile(3 + place)
        down, across = pl.ds(row * EDGE, EDGE), pl.ds(column * EDGE, EDGE)
        gram_ref[down, across] = block
        gram_ref[across, down] = block.T
    squares = jnp.sum(jnp.sum(squares, axis=0, keepdims=True), axis=1, keepdims=True)
    inv_norm = 1.0 / (jnp.sqrt(squares) + norm_epsilon)
    inv_square = inv_norm * inv_norm

    factor = gram_ref[...]
    half = factor.shape[0] // 2
    coupling = [
        factor[:half].astype(jnp.float32) * inv_square,
        factor[half:, half:].astype(jnp.float32) * inv_square,
    ]
    square = symmetric_product([factor], factor)
    third = quintic_third * (inv_square * inv_square)
    step = [quintic_second * c + third * s for c, s in zip(coupling, square)]
    step = two_parts(whole(*step))
    operand = owned_ref[...]
    product = [p * inv_square for p in symmetric_product(step, factor)]
    current = (quintic_first * operand.astype(jnp.float32) + matmul(step[0], operand)) * inv_norm
    rest_scale = inv_norm
    for iteration in range(1, ITERS):
        high, low = two_parts(whole(*product))
        coupling = [
            quintic_first * quintic_first * c + 2.0 * quintic_first * p + (d + e)
            for c, p, d, e in zip(
                coupling, product, symmetric_product(step, high), symmetric_product(step[:1], low)
            )
        ]
        current = current + matmul(step[1], operand) * rest_scale
        operand = current.astype(jnp.bfloat16)
        factor = whole(*coupling).astype(jnp.bfloat16)
        if iteration + 1 < ITERS:
            square = symmetric_product([factor], factor)
            step = [quintic_second * c + quintic_third * s for c, s in zip(coupling, square)]
            step = two_parts(whole(*step))
            product = symmetric_product(step, factor)
            current = quintic_first * current + matmul(step[0], operand)
            rest_scale = 1.0
    first = matmul(factor, operand).astype(jnp.bfloat16)
    for rows in (slice(0, half), slice(half, 2 * half)):
        second = matmul(factor[rows], first)
        update = quintic_first * current[rows] + quintic_second * first[rows].astype(jnp.float32) + quintic_third * second
        update_ref[rows, :] = (scale_out * update).astype(jnp.bfloat16)


def gather_kernel(order_ref, source_ref, slots_ref):
    def body(slot, carry):
        slots_ref[slot] = source_ref[order_ref[slot]]
        return carry

    lax.fori_loop(0, slots_ref.shape[0], body, 0, unroll=8)


def master_kernel(order_ref, returned_ref, master_ref, update_ref, out_ref, owned_ref, ready_ref, sem, owned_sem):
    owned = pltpu.make_async_copy(update_ref, owned_ref, owned_sem)
    owned.start()

    def body(slot, carry):
        matrix = order_ref[slot]
        ready_ref[matrix] = master_ref[matrix] * (1.0 - learn_rate * weight_decay) - learn_rate * returned_ref[
            slot
        ].astype(jnp.float32)
        pltpu.make_async_copy(ready_ref.at[matrix], out_ref.at[matrix], sem).start()
        return carry

    lax.fori_loop(0, returned_ref.shape[0], body, 0, unroll=4)
    pltpu.make_async_copy(ready_ref, out_ref, sem).wait()
    owned.wait()


def limit(mib):
    return pltpu.CompilerParams(vmem_limit_bytes=mib * 1024 * 1024)


def vmem():
    return pl.BlockSpec(memory_space=pltpu.VMEM)


def smem():
    return pl.BlockSpec(memory_space=pltpu.SMEM)


def shards(chips, momentum, master, owner_order):
    matrices, rows, columns = momentum.shape
    slots = matrices
    core = lax.axis_index("core").astype(jnp.int32).reshape(1)
    swap = ((0, 1), (1, 0))
    slotted = pl.pallas_call(
        gather_kernel,
        out_shape=jax.ShapeDtypeStruct(momentum.shape, momentum.dtype),
        in_specs=[smem(), vmem()],
        out_specs=vmem(),
        compiler_params=limit(53),
        name="gather",
    )(pltpu.with_memory_space_constraint(owner_order, pltpu.HBM), momentum)
    core, slotted = lax.optimization_barrier((core, slotted))
    owned = lax.all_to_all(slotted, "dp", split_axis=0, concat_axis=0, tiled=True)
    owned = owned.reshape(slots * rows, columns)
    packed = jax.ShapeDtypeStruct((HALF_ROWS, EDGE), jnp.bfloat16)
    kept, sent = pl.pallas_call(
        gram_kernel,
        out_shape=(packed, packed),
        in_specs=[smem(), vmem()],
        out_specs=(vmem(), vmem()),
        scratch_shapes=[pltpu.VMEM((2 * HALF_ROWS, EDGE), jnp.bfloat16)],
        compiler_params=limit(8),
        name="gram",
    )(core, owned)
    received = lax.ppermute(sent, "core", swap)
    pair = (kept.astype(jnp.float32) + received.astype(jnp.float32)).astype(jnp.bfloat16)
    pair = pair.reshape(chips, HALF_ROWS // chips, EDGE)
    parts = lax.all_to_all(pair, "x", split_axis=0, concat_axis=0, tiled=True)
    spread = pl.pallas_call(
        sum_kernel,
        out_shape=jax.ShapeDtypeStruct(parts.shape, jnp.bfloat16),
        in_specs=[vmem()],
        out_specs=vmem(),
        compiler_params=limit(4),
        name="sum",
    )(parts)
    mine = lax.all_to_all(spread, "x", split_axis=0, concat_axis=0, tiled=True)
    mine = mine.reshape(HALF_ROWS, EDGE)
    other = lax.ppermute(mine, "core", swap)
    edge = owned.shape[0]
    update = pl.pallas_call(
        update_kernel,
        out_shape=jax.ShapeDtypeStruct(owned.shape, jnp.bfloat16),
        in_specs=[smem(), vmem(), vmem(), vmem()],
        out_specs=vmem(),
        scratch_shapes=[
            pltpu.VMEM((2 * HALF_ROWS, EDGE), jnp.bfloat16),
            pltpu.VMEM((edge, edge), jnp.bfloat16),
        ],
        compiler_params=limit(24),
        name="update",
    )(core, mine, other, owned)
    returned = lax.all_to_all(
        update.reshape(slots, rows, columns), "dp", split_axis=0, concat_axis=0, tiled=True
    )
    new_master, owned_update = pl.pallas_call(
        master_kernel,
        out_shape=(
            jax.ShapeDtypeStruct(master.shape, jnp.float32),
            jax.ShapeDtypeStruct(update.shape, update.dtype),
        ),
        in_specs=[smem(), vmem(), vmem(), vmem()],
        out_specs=(pl.BlockSpec(memory_space=pl.ANY),) * 2,
        scratch_shapes=[
            pltpu.VMEM(master.shape, jnp.float32),
            pltpu.SemaphoreType.DMA,
            pltpu.SemaphoreType.DMA,
        ],
        compiler_params=limit(8),
        name="master",
    )(owner_order, returned, master, update)
    return (new_master, owned_update[None])


def solution(mesh):
    owners, columns = mesh.devices.shape
    chips = columns // 2
    split = Mesh(mesh.devices.reshape(owners, chips, 2), ("dp", "x", "core"))
    tensor = ("x", "core")
    return jax.shard_map(
        functools.partial(shards, chips),
        mesh=split,
        in_specs=(P(None, "dp", tensor), P(None, "dp", tensor), P()),
        out_specs=(P(None, "dp", tensor), P("dp", None, tensor)),
        check_vma=False,
    )
```
